256 devices in a mesh: tile: 64 (over x, z, core), lev: 4 (over y).
Axes of the slice: x: 4, y: 4, z: 8, core: 2. Of those that a mesh axis runs over, the one named last changes fastest.
Arguments:
- fields: float32 [2, 60, 8192, 128], P(None, 'lev', 'tile'), may hold values from -6 to 6
- wind_x: float32 [60, 8192, 128], P('lev', 'tile'), may hold values from -0.8 to 0.8
- wind_y: float32 [60, 8192, 128], P('lev', 'tile'), may hold values from -0.8 to 0.8
- diffusivity: float32 [60, 8192, 128], P('lev', 'tile'), may hold values from 0.02 to 0.3
- surface: float32 [8, 1048576], P(None, ('tile', 'lev')), may hold values from -6 to 6
- cloud_list: int32 [1048576], P(('tile', 'lev')), may hold values from -1 to 4095, as said below
- input_weight: bfloat16 [128, 512], replicated, may hold values from -0.5 to 0.5
- hidden_weight: bfloat16 [5, 512, 512], replicated, may hold values from -0.25 to 0.25
- output_weight: bfloat16 [512, 128], replicated, may hold values from -0.25 to 0.25
- clear_weight: bfloat16 [128, 128], replicated, may hold values from -0.5 to 0.5
Outputs:
- fields_out: float32 [2, 60, 1048576], P(None, None, ('tile', 'lev'))
- surface_out: float32 [8, 1048576], P(None, ('tile', 'lev'))
The draws below stay inside these ranges and needn't reach their ends.
Inputs may be any that keep to these rules, and one draw needn't show every extreme that they name: `cloud_list`: block d of 4096 entries belongs to the device of tile index d // 4 and lev index d % 4, whose columns are d * 4096 onward. Each block lists distinct local indices of cloudy columns in any order, then -1 to its end. Over the 64 blocks of one lev index, the numbers ceil(cloudy count / 64) sum to more than (31) * 64 and at most 2048.
All inputs are finite; a program needn't handle non-finite values.
Results may differ from the reference program's by a relative error of at most 0.0055.
Values may be sent and summed in bfloat16 or wider, within the bound.
No kernel may reach another device: no remote copies, remote signals or barrier semaphores. Data moves between devices by JAX's collectives and lax.ppermute only.
A program may use at most 128 MiB of HBM per device.

```python
import math
import jax
import jax.numpy as jnp
from jax import lax

LEVELS = 60
SURF = 8
HID = 512
HIDDEN_LAYERS = 5
NY = 128
F_IN = 128
NX = 8192
COLUMNS = 1048576
COLS_DEV = 4096
BLOCK = 64
RECV_MOST = 32
N_TILE = 64
N_LEV = 4


def draw_cloud_list(key, part):
    tile_count = N_TILE
    groups = N_LEV
    cells = tile_count * tile_count
    keys = jax.random.split(jax.random.fold_in(key, 7), 5)
    weights = jax.random.randint(keys[0], (groups, tile_count, 1), 0, 3)
    orders = jax.vmap(lambda sub: jax.random.permutation(sub, cells))(jax.random.split(keys[1], groups))
    orders = orders.reshape(groups, tile_count, tile_count)
    cell_ids = jnp.arange(cells, dtype=jnp.int32).reshape(1, tile_count, tile_count)
    scores = (weights * (cells // 2) + orders) * cells + cell_ids
    ranking = jnp.argsort(jnp.argsort(scores.reshape(groups, cells), axis=1), axis=1)
    totals = RECV_MOST * tile_count - jax.random.randint(keys[2], (groups, 1), 0, tile_count)
    chosen = (ranking < totals).astype(jnp.int32).reshape(groups, tile_count, tile_count)
    block_counts = jnp.sum(chosen, axis=2)
    last_fill = jax.random.randint(keys[3], (groups, tile_count), 1, BLOCK + 1)
    cloudy_counts = jnp.where(block_counts > 0, (block_counts - 1) * BLOCK + last_fill, 0)
    picks = jax.vmap(lambda sub: jax.random.permutation(sub, COLS_DEV))(jax.random.split(keys[4], groups * tile_count))
    picks = picks.reshape(tile_count, groups, COLS_DEV)
    positions = jnp.arange(COLS_DEV, dtype=jnp.int32).reshape(1, 1, COLS_DEV)
    listed = jnp.where(positions < cloudy_counts.T[:, :, None], picks, -1)
    return listed.reshape(-1).astype(jnp.int32)


def level_of(stream_key, dims, pieces, smallest, top_value):
    gain = 1.0
    for dim, parts in pieces:
        heights = jax.random.uniform(jax.random.fold_in(jax.random.fold_in(stream_key, 6), dim), (parts,), jnp.float32, smallest / len(pieces), top_value / len(pieces))
        gain = gain * jnp.repeat(jnp.exp(heights), dims[dim] // parts).reshape((-1,) + (1,) * (len(dims) - 1 - dim))
    return gain


def centred(rng, dims, scale, most, pieces=(), kind=jnp.bfloat16):
    array = jax.random.normal(rng, dims, jnp.float32) * scale
    if len(pieces) > 0:
        array = level_of(rng, dims, pieces, -0.22, 0.18) * array
    return jnp.clip(array, min=-most, max=most).astype(kind)


def setup_inputs(seed: int = 0) -> dict:
    key_of = jax.random.split(jax.random.key(seed), 11)
    return {
        "fields": centred(key_of[0], (2, LEVELS, NX, NY), 1.0, 6.0, ((1, 4), (2, 64)), jnp.float32),
        "wind_x": jnp.clip(jax.random.uniform(key_of[1], (LEVELS, NX, NY), jnp.float32, -0.8, 0.8) * level_of(key_of[1], (LEVELS, NX, NY), ((0, 4), (1, 64)), -0.4, 0.0), -0.8, 0.8),
        "wind_y": jnp.clip(jax.random.uniform(key_of[2], (LEVELS, NX, NY), jnp.float32, -0.8, 0.8) * level_of(key_of[2], (LEVELS, NX, NY), ((0, 4), (1, 64)), -0.4, 0.0), -0.8, 0.8),
        "diffusivity": jnp.clip(jnp.exp(math.log(0.3) - 2.7080503 * jax.random.uniform(key_of[3], (LEVELS, NX, NY), jnp.float32) ** level_of(key_of[3], (LEVELS, NX, NY), ((0, 4), (1, 64)), -0.2, 0.2)), 0.02, 0.3),
        "surface": centred(key_of[4], (SURF, COLUMNS), 1.0, 6.0, ((1, 256),), jnp.float32),
        "cloud_list": draw_cloud_list(jax.random.fold_in(key_of[10], 71), 0),
        "input_weight": centred(key_of[6], (F_IN, HID), F_IN ** -0.5, 0.5),
        "hidden_weight": centred(key_of[7], (HIDDEN_LAYERS, HID, HID), HID ** -0.5, 0.25),
        "output_weight": centred(key_of[8], (HID, F_IN), HID ** -0.5, 0.25),
        "clear_weight": centred(key_of[9], (F_IN, F_IN), F_IN ** -0.5, 0.5),
    }


def rate(field, wind_east, wind_north, diffuse):
    east_cell = jnp.roll(field, -1, axis=2)
    west_cell = jnp.roll(field, 1, axis=2)
    zero_edge = jnp.zeros_like(field[..., :1])
    north_cell = jnp.concatenate([field[..., 1:], zero_edge], axis=-1)
    south_cell = jnp.concatenate([zero_edge, field[..., :-1]], axis=-1)
    spread = east_cell + west_cell + north_cell + south_cell - 4.0 * field
    carried = wind_east * (east_cell - west_cell) + wind_north * (north_cell - south_cell)
    return diffuse * spread - 0.5 * carried


def physics_rows(batch, input_weight, hidden_weight, output_weight):
    stream = jax.nn.silu(jnp.dot(batch.astype(jnp.float32), input_weight.astype(jnp.float32)))
    for layer_index in range(HIDDEN_LAYERS):
        operand = stream.astype(jnp.bfloat16).astype(jnp.float32)
        stream = stream + jax.nn.silu(jnp.dot(operand, hidden_weight[layer_index].astype(jnp.float32)))
    operand = stream.astype(jnp.bfloat16).astype(jnp.float32)
    return jnp.dot(operand, output_weight.astype(jnp.float32)).astype(jnp.bfloat16)


def reference(fields, wind_x, wind_y, diffusivity, surface, cloud_list, input_weight, hidden_weight, output_weight, clear_weight):
    section_one = fields + rate(fields, wind_x, wind_y, diffusivity) / 3.0
    section_two = fields + 0.5 * rate(section_one, wind_x, wind_y, diffusivity)
    advected = fields + rate(section_two, wind_x, wind_y, diffusivity)
    columns = advected.reshape(2, LEVELS, COLUMNS)
    features = jnp.concatenate([columns.reshape(2 * LEVELS, COLUMNS), surface], axis=0).astype(jnp.bfloat16).T
    clear_part = jnp.dot(features.astype(jnp.float32), clear_weight.astype(jnp.float32))
    base_index = (jnp.arange(COLUMNS, dtype=jnp.int32) // COLS_DEV) * COLS_DEV
    target = jnp.where(cloud_list >= 0, base_index + cloud_list, COLUMNS).astype(jnp.int32)
    cloudy = jnp.zeros((COLUMNS + 1,), dtype=jnp.int32).at[target].set(1)[:COLUMNS]
    physics = lax.map(lambda batch: physics_rows(batch, input_weight, hidden_weight, output_weight),
                      features.reshape(COLUMNS // COLS_DEV, COLS_DEV, F_IN)).reshape(COLUMNS, F_IN)
    tendency = (clear_part + jnp.where(cloudy[:, None] > 0, physics.astype(jnp.float32), 0.0)).astype(jnp.bfloat16)
    tend_cols = tendency.astype(jnp.float32).T
    fields_out = columns + tend_cols[:2 * LEVELS].reshape(2, LEVELS, COLUMNS)
    surface_out = surface + tend_cols[2 * LEVELS:]
    return fields_out, surface_out
```

```python
import functools

import jax
import jax.numpy as jnp
from jax import lax
from jax.experimental import pallas as pl
from jax.experimental.pallas import tpu as pltpu
from jax.sharding import PartitionSpec as P

VARS = 2
GROUP = 15
LEVELS = 60
SURF = 8
ROWS = 128
NY = 128
OWN = 32
PAD = 16
HID = 512
OUT_ROWS = 136
KEYS = 144
CHUNKS = (((8, 16),), ((0, 8), (24, 8)))
COLS_STEP = 512


def ring(count, shift):
    return [(i, (i + shift) % count) for i in range(count)]


def regions_of(chunk):
    rows = []
    for owner in range(ROWS // OWN):
        for start, size in chunk:
            for off in range(0, size, 8):
                rows.append(owner * OWN + start + off)
    regions = []
    for row in rows:
        if regions and regions[-1][1] == row:
            regions[-1][1] = row + 8
        else:
            regions.append([row, row + 8])
    return regions


def stencil_kernel(chunk, with_halo, *refs):
    if with_halo:
        lev_ref, field_ref, wx_ref, wy_ref, d_ref, lo_ref, hi_ref, out_ref, f_s, s1_s, s2_s, c_s = refs
    else:
        lev_ref, field_ref, wx_ref, wy_ref, d_ref, out_ref, f_s, s1_s, s2_s, c_s = refs
    lev = lev_ref[0]
    lane = lax.broadcasted_iota(jnp.int32, (GROUP, NY), 1)
    row_ok = lax.broadcasted_iota(jnp.int32, (PAD, NY), 0) < GROUP
    place = {}
    for owner in range(ROWS // OWN):
        at = 0
        for start, size in chunk:
            for off in range(0, size, 8):
                place[owner * OWN + start + off] = (owner, at)
                at += 8

    def put_coefs(i, wx, wy, d):
        hx = 0.5 * wx
        hy = 0.5 * wy
        c_s[0, i, 0:GROUP] = d - hx
        c_s[1, i, 0:GROUP] = d + hx
        c_s[2, i, 0:GROUP] = jnp.where(lane == NY - 1, 0.0, d - hy)
        c_s[3, i, 0:GROUP] = jnp.where(lane == 0, 0.0, d + hy)
        c_s[4, i, 0:GROUP] = 4.0 * d

    def load_inner(i, x, coefs):
        for v in range(VARS):
            f_s[i, v * PAD : v * PAD + GROUP] = field_ref[pl.ds(v * GROUP * ROWS + x, GROUP, stride=ROWS), :]
        if coefs:
            at = pl.ds(x, GROUP, stride=ROWS)
            put_coefs(i, wx_ref[at, :], wy_ref[at, :], d_ref[at, :])

    def load_halo(i, ref, far, near):
        for v in range(VARS):
            f_s[i, v * PAD : v * PAD + GROUP] = ref[pl.ds(v * GROUP * 3 + far, GROUP, stride=3), :]
        if near is not None:
            w = [ref[pl.ds(VARS * GROUP * 3 + k * GROUP * 2 + near, GROUP, stride=2), :] for k in range(3)]
            put_coefs(i, *w)

    def section(src, i, v):
        part = pl.ds(v * PAD, PAD)
        mid = src[i, part]
        total = c_s[0, i] * src[i + 1, part] + c_s[1, i] * src[i - 1, part]
        total = total + c_s[2, i] * pltpu.roll(mid, NY - 1, 1) + c_s[3, i] * pltpu.roll(mid, 1, 1)
        return total - c_s[4, i] * mid

    for a, b in regions_of(chunk):
        n = b - a
        first, last = 0, n + 6
        if a == 0:
            for k in range(3):
                load_halo(k, lo_ref, k, k - 1 if k >= 1 else None)
            first = 3
        if b == ROWS:
            for k in range(3):
                load_halo(n + 3 + k, hi_ref, k, k if k < 2 else None)
            last = n + 3

        def fill(i, _, a=a):
            load_inner(i, a - 3 + i, True)
            return 0

        lax.fori_loop(first, last, fill, 0, unroll=2)

        def one(i, _):
            for v in range(VARS):
                part = pl.ds(v * PAD, PAD)
                s1_s[i, part] = f_s[i, part] + section(f_s, i, v) * (1.0 / 3.0)
            return 0

        lax.fori_loop(1, n + 5, one, 0, unroll=2)

        def two(i, _):
            for v in range(VARS):
                part = pl.ds(v * PAD, PAD)
                s2_s[i, part] = f_s[i, part] + section(s1_s, i, v) * 0.5
            return 0

        lax.fori_loop(2, n + 4, two, 0, unroll=2)

        for off in range(0, n, 8):
            owner, at = place[a + off]
            slot = lax.rem(owner - lev + 4, 4)

            def three(k, _, off=off, slot=slot, at=at):
                i = 3 + off + k
                parts = []
                for v in range(VARS):
                    part = pl.ds(v * PAD, PAD)
                    value = f_s[i, part] + section(s2_s, i, v)
                    parts.append(jnp.where(row_ok, value, 0.0).astype(jnp.bfloat16))
                out_ref[slot, at + k, 0:PAD] = parts[0]
                out_ref[slot, at + k, PAD : 2 * PAD] = parts[1]
                return 0

            lax.fori_loop(0, 8, three, 0, unroll=2)


def stencil(chunk, lev, flat_fields, winds, halo):
    rows = sum(size for _, size in chunk)
    most = max(b - a for a, b in regions_of(chunk)) + 6
    vmem = pl.BlockSpec(memory_space=pltpu.VMEM)
    operands = [lev, flat_fields, *winds, *halo]
    return pl.pallas_call(
        functools.partial(stencil_kernel, chunk, len(halo) > 0),
        out_shape=jax.ShapeDtypeStruct((4, rows, 2 * PAD, NY), jnp.bfloat16),
        in_specs=[pl.BlockSpec(memory_space=pltpu.SMEM)] + [vmem] * (len(operands) - 1),
        out_specs=vmem,
        scratch_shapes=[
            pltpu.VMEM((most, 2 * PAD, NY), jnp.float32),
            pltpu.VMEM((most, 2 * PAD, NY), jnp.float32),
            pltpu.VMEM((most, 2 * PAD, NY), jnp.float32),
            pltpu.VMEM((5, most, PAD, NY), jnp.float32),
        ],
        name="stencil",
    )(*operands)


def prep_kernel(lev_ref, list_ref, win_ref, wh_ref, wo_ref, wc_ref, cat_ref, wht_ref, wot_ref, mask_ref):
    lev = lev_ref[0]
    f32 = jnp.float32
    bf16 = jnp.bfloat16
    f_id = lax.broadcasted_iota(jnp.int32, (OUT_ROWS, 128), 1)
    o_id = lax.broadcasted_iota(jnp.int32, (OUT_ROWS, 128), 0)
    var = (f_id >= LEVELS).astype(jnp.int32) + (f_id >= 2 * LEVELS).astype(jnp.int32)
    u = (o_id == f_id + 4 * var).astype(f32).astype(bf16)
    k_id = lax.broadcasted_iota(jnp.int32, (OUT_ROWS, KEYS), 1)
    o_id = lax.broadcasted_iota(jnp.int32, (OUT_ROWS, KEYS), 0)
    source = (lev - (k_id >> 5) + 4) & 3
    level = source * GROUP + (k_id & 15)
    row = ((k_id >> 4) & 1) * 64 + level
    inner = (k_id < 128) & ((k_id & 15) < GROUP) & (o_id == row)
    edge = (k_id >= 128) & (o_id == k_id)
    r = (inner | edge).astype(f32).astype(bf16)
    nt = (((1,), (1,)), ((), ()))
    tn = (((0,), (0,)), ((), ()))
    ur = lax.dot_general(u, r, tn, preferred_element_type=f32).astype(bf16)
    cat_ref[0:HID] = (0.5 * lax.dot_general(win_ref[...], ur, tn, preferred_element_type=f32)).astype(bf16)
    clear = lax.dot_general(wc_ref[...], ur, tn, preferred_element_type=f32).astype(bf16)
    cat_ref[HID : HID + OUT_ROWS] = jnp.dot(u, clear, preferred_element_type=f32).astype(bf16)
    cat_ref[HID + OUT_ROWS :] = r[0:128]
    wot_ref[...] = lax.dot_general(u, wo_ref[...], nt, preferred_element_type=f32).astype(bf16)
    for l in range(wh_ref.shape[0]):
        wht_ref[l] = (0.5 * wh_ref[l].astype(f32).T).astype(bf16)
    e = list_ref[...]
    hi = lax.broadcasted_iota(jnp.int32, (OWN, e.shape[1]), 0) == (e >> 7)
    lo = lax.broadcasted_iota(jnp.int32, (128, e.shape[1]), 0) == (e & 127)
    mask_ref[...] = lax.dot_general(
        hi.astype(f32).astype(bf16), lo.astype(f32).astype(bf16), nt, preferred_element_type=f32
    )


def prep(lev, cloud_list, input_weight, hidden_weight, output_weight, clear_weight):
    vmem = pl.BlockSpec(memory_space=pltpu.VMEM)
    return pl.pallas_call(
        prep_kernel,
        out_shape=(
            jax.ShapeDtypeStruct((HID + OUT_ROWS + 128, KEYS), jnp.bfloat16),
            jax.ShapeDtypeStruct(hidden_weight.shape, jnp.bfloat16),
            jax.ShapeDtypeStruct((OUT_ROWS, HID), jnp.bfloat16),
            jax.ShapeDtypeStruct((OWN, 128), jnp.float32),
        ),
        in_specs=[pl.BlockSpec(memory_space=pltpu.SMEM)] + [vmem] * 5,
        out_specs=(vmem,) * 4,
        name="prep",
    )(lev, cloud_list.reshape(1, -1), input_weight, hidden_weight, output_weight, clear_weight)


def physics_kernel(chunk, g0, g1, g2, g3, surf_ref, cat_ref, wht_ref, wot_ref, mask_ref, *rest):
    out_ref, surf_out_ref, s_ref, b_ref = rest[-4:]
    step = pl.program_id(0)
    f32 = jnp.float32
    bf16 = jnp.bfloat16
    halves = COLS_STEP // 256
    block = jnp.int32(0)
    at = 0
    for start, size in chunk:
        block = jnp.where(step >= at, step - at + start // 4, block)
        at += size // 4
    layers = wht_ref.shape[0]
    clear = []
    columns = []
    surf = []

    def act(a):
        return a + a * jnp.tanh(a)

    for h in range(halves):
        cols = slice(256 * h, 256 * h + 256)
        pieces = [jnp.concatenate([g[2 * h], g[2 * h + 1]], axis=1) for g in (g0, g1, g2, g3)]
        sf = surf_ref[:, cols]
        surf.append(sf)
        pieces.append(jnp.concatenate([sf, jnp.zeros_like(sf)], axis=0).astype(bf16))
        x = jnp.concatenate(pieces, axis=0)
        a = jnp.dot(cat_ref[0:HID], x, preferred_element_type=f32)
        s = act(a)
        s_ref[h] = s
        b_ref[0, h] = s.astype(bf16)
        tail = jnp.dot(cat_ref[HID:], x, preferred_element_type=f32)
        clear.append(tail[0:OUT_ROWS])
        columns.append(tail[OUT_ROWS:])
    for l in range(layers):
        for h in range(halves):
            a = jnp.dot(wht_ref[l], b_ref[l % 2, h], preferred_element_type=f32)
            s = s_ref[h] + act(a)
            if l + 1 < layers:
                s_ref[h] = s
            b_ref[(l + 1) % 2, h] = s.astype(bf16)
    for h in range(halves):
        cols = slice(256 * h, 256 * h + 256)
        o = jnp.dot(wot_ref[...], b_ref[layers % 2, h], preferred_element_type=f32)
        o = o.astype(bf16).astype(f32)
        keep = jnp.concatenate(
            [mask_ref[pl.ds(block * 4 + 2 * h + k, 1), :] for k in range(2)], axis=1
        )
        tend = (clear[h] + jnp.where(keep > 0.5, o, 0.0)).astype(bf16).astype(f32)
        total = columns[h] + tend[0:128]
        out_ref[0, :, cols] = total[0:LEVELS]
        out_ref[1, :, cols] = total[64 : 64 + LEVELS]
        surf_out_ref[:, cols] = surf[h] + tend[128:]


def physics(chunk, got, surface, cat, wht, wot, mask, previous):
    rows = sum(size for _, size in chunk)
    steps = rows // 4

    def block_of(i):
        block = i + chunk[0][0] // 4
        at = 0
        for start, size in chunk:
            block = jnp.where(i >= at, i - at + start // 4, block)
            at += size // 4
        return block

    whole = lambda a: pl.BlockSpec(a.shape, lambda i: (0,) * a.ndim)
    g_spec = pl.BlockSpec((4, 2 * PAD, NY), lambda i: (i, 0, 0))
    s_spec = pl.BlockSpec((SURF, COLS_STEP), lambda i: (0, block_of(i)))
    o_spec = pl.BlockSpec((VARS, LEVELS, COLS_STEP), lambda i: (0, 0, block_of(i)))
    in_specs = [g_spec] * 4 + [s_spec, whole(cat), whole(wht), whole(wot), whole(mask)]
    operands = [*got, surface, cat, wht, wot, mask]
    aliases = {}
    if previous is not None:
        aliases = {len(operands): 0, len(operands) + 1: 1}
        in_specs += [pl.BlockSpec(memory_space=pl.ANY)] * 2
        operands += list(previous)
    columns = surface.shape[1]
    return pl.pallas_call(
        functools.partial(physics_kernel, chunk),
        grid=(steps,),
        out_shape=(
            jax.ShapeDtypeStruct((VARS, LEVELS, columns), jnp.float32),
            jax.ShapeDtypeStruct((SURF, columns), jnp.float32),
        ),
        in_specs=in_specs,
        out_specs=(o_spec, s_spec),
        scratch_shapes=[
            pltpu.VMEM((COLS_STEP // 256, HID, 256), jnp.float32),
            pltpu.VMEM((2, COLS_STEP // 256, HID, 256), jnp.bfloat16),
        ],
        input_output_aliases=aliases,
        name="physics",
    )(*operands)


def local(
    fields,
    wind_x,
    wind_y,
    diffusivity,
    surface,
    cloud_list,
    input_weight,
    hidden_weight,
    output_weight,
    clear_weight,
):
    tiles = lax.axis_size("tile")
    levs = lax.axis_size("lev")
    lev = lax.axis_index("lev").astype(jnp.int32).reshape(1)

    def edge(far, near):
        parts = [fields[:, :, far].reshape(-1, NY)]
        parts += [a[:, near].reshape(-1, NY) for a in (wind_x, wind_y, diffusivity)]
        return jnp.concatenate(parts, axis=0)

    lo = lax.ppermute(edge(slice(ROWS - 3, None), slice(ROWS - 2, None)), "tile", ring(tiles, 1))
    hi = lax.ppermute(edge(slice(0, 3), slice(0, 2)), "tile", ring(tiles, -1))
    flat = fields.reshape(-1, NY)
    winds = [a.reshape(-1, NY) for a in (wind_x, wind_y, diffusivity)]
    sends = [stencil(CHUNKS[0], lev, flat, winds, []), stencil(CHUNKS[1], lev, flat, winds, [lo, hi])]
    weights = prep(lev, cloud_list, input_weight, hidden_weight, output_weight, clear_weight)
    out = None
    for chunk, send in zip(CHUNKS, sends):
        got = [send[0]] + [lax.ppermute(send[s], "lev", ring(levs, s)) for s in range(1, levs)]
        cat, wht, wot, mask = weights
        out = physics(chunk, got, surface, cat, wht, wot, mask, out)
    return out


def solution(mesh):
    return jax.shard_map(
        local,
        mesh=mesh,
        in_specs=(
            P(None, "lev", "tile", None),
            P("lev", "tile", None),
            P("lev", "tile", None),
            P("lev", "tile", None),
            P(None, ("tile", "lev")),
            P(("tile", "lev")),
            P(),
            P(),
            P(),
            P(),
        ),
        out_specs=(P(None, None, ("tile", "lev")), P(None, ("tile", "lev"))),
        check_vma=False,
    )
```

```python
import functools

import jax
import jax.numpy as jnp
from jax import lax
from jax.experimental import pallas as pl
from jax.experimental.pallas import tpu as pltpu
from jax.sharding import PartitionSpec as P


VARS = 2
GROUP = 15
LEVELS = 60
SURF = 8
ROWS = 128
NY = 128
OWN = 32
PAD = 16
HID = 512
HALF = 1024
OUT_ROWS = 136
KEYS = 144
CHUNKS = ((8, 16), (0, 24))
HALO = 192
MIB = 1 << 20
EDGES_GRANT = 60 * MIB
INNER_GRANT = 60 * MIB


def ring(count, shift):
    return [(i, (i + shift) % count) for i in range(count)]


def edges_kernel(*refs):
    arrays, halos, buffers, sems = refs[:4], refs[4:6], refs[6:14], refs[14]
    copies = []
    for side in range(2):
        for k, a in enumerate(arrays):
            rows = pl.ds(0 if side else ROWS - 8, 8)
            copies.append(pltpu.make_async_copy(a.at[:, rows], buffers[4 * side + k], sems.at[4 * side + k]))
    for copy in copies:
        copy.start()
    for copy in copies:
        copy.wait()
    for side in range(2):
        fields, winds, out = buffers[4 * side], buffers[4 * side + 1 : 4 * side + 4], halos[side]
        far, near = (5, 6) if side == 0 else (0, 0)
        flat = fields.reshape(VARS * GROUP * 8, NY)
        for k in range(3):
            for v in range(VARS):
                at = 32 * k + PAD * v
                out[at : at + GROUP] = flat[pl.ds(v * GROUP * 8 + far + k, GROUP, stride=8), :]
        for j, wind in enumerate(winds):
            flat = wind.reshape(GROUP * 8, NY)
            for k in range(2):
                at = 96 + 48 * k + PAD * j
                out[at : at + GROUP] = flat[pl.ds(near + k, GROUP, stride=8), :]


def edges(fields, winds):
    arrays = (fields, *winds)
    vmem = pl.BlockSpec(memory_space=pltpu.VMEM)
    halo = jax.ShapeDtypeStruct((HALO, NY), jnp.float32)
    ends = [jax.ShapeDtypeStruct((a.shape[0], 8, NY), jnp.float32) for a in arrays + arrays]
    return pl.pallas_call(
        edges_kernel,
        out_shape=(halo, halo, *ends),
        in_specs=[pl.BlockSpec(memory_space=pl.ANY)] * 4,
        out_specs=(vmem,) * 10,
        scratch_shapes=[pltpu.SemaphoreType.DMA((8,))],
        compiler_params=pltpu.CompilerParams(vmem_limit_bytes=EDGES_GRANT),
        name="edges",
    )(*arrays)


def coefs_of(wx, wy, d):
    lane = lax.broadcasted_iota(jnp.int32, (GROUP, NY), 1)
    hx = 0.5 * wx
    hy = 0.5 * wy
    north = jnp.where(lane == NY - 1, 0.0, d - hy)
    south = jnp.where(lane == 0, 0.0, d + hy)
    return d - hx, d + hx, north, south, 4.0 * d


def put_coefs(c_s, i, winds):
    for k, c in enumerate(coefs_of(*winds)):
        c_s[i, k, 0:GROUP] = c


def get_rows(refs, rows, x):
    flat = refs[0].reshape(VARS * GROUP * rows, NY)
    fields = [flat[pl.ds(v * GROUP * rows + x, GROUP, stride=rows), :] for v in range(VARS)]
    winds = [w.reshape(GROUP * rows, NY)[pl.ds(x, GROUP, stride=rows), :] for w in refs[1:]]
    return fields, winds


def put_fields(f_s, i, fields):
    for v in range(VARS):
        f_s[i, v, 0:GROUP] = fields[v]


def rate(cs, west, mid, east):
    total = cs[0] * east + cs[1] * west
    total = total + cs[2] * pltpu.roll(mid, NY - 1, 1) + cs[3] * pltpu.roll(mid, 1, 1)
    return total - cs[4] * mid


def sweep(f_s, s1_s, s2_s, c_s, base, count, first, write):
    levels = ((f_s, s1_s, 1.0 / 3.0), (s1_s, s2_s, 0.5), (s2_s, None, 1.0))
    for stage, (src, dst, scale) in enumerate(levels):
        low, high = first[stage], first[stage] + count[stage]
        held = {}

        def row(i, v):
            if (i, v) not in held:
                held[i, v] = src[base + i, v]
            return held[i, v]

        for i in range(low, high):
            cs = [c_s[base + i, k] for k in range(5)]
            for v in range(VARS):
                value = rate(cs, row(i - 1, v), row(i, v), row(i + 1, v))
                if scale != 1.0:
                    value = value * scale
                value = f_s[base + i, v] + value
                if dst is None:
                    write(i, v, value)
                else:
                    dst[base + i, v] = value
                held.pop((i - 1, v))


def masked(value):
    ok = lax.broadcasted_iota(jnp.int32, (PAD, NY), 0) < GROUP
    return jnp.where(ok, value, 0.0).astype(jnp.bfloat16)


def inner_kernel(lev_ref, *refs):
    arrays, outs, buffers = refs[:4], refs[4:12], refs[12:16]
    f_s, s1_s, s2_s, c_s, o_s, sems = refs[16:]
    parts = 4
    size = ROWS // parts

    def copies(part):
        rows = pl.ds(pl.multiple_of(part * size, size), size)
        return [
            pltpu.make_async_copy(a.at[:, rows], b.at[:, rows], sems.at[part, k])
            for k, (a, b) in enumerate(zip(arrays, buffers))
        ]

    for part in range(2):
        for copy in copies(part):
            copy.start()

    def one(block, _):
        part = lax.div(block, parts)

        @pl.when(lax.rem(block, parts) == 0)
        def _():
            for copy in copies(part):
                copy.wait()

            @pl.when(part + 2 < parts)
            def _():
                for copy in copies(part + 2):
                    copy.start()

        base = 8 * block
        for i in range(8):
            fields, winds = get_rows(buffers, ROWS, base + i)
            put_fields(f_s, 8 + i, fields)
            put_coefs(c_s, 8 + i, winds)

        def write(i, v, value):
            o_s[base + i, v] = masked(value)

        sweep(f_s, s1_s, s2_s, c_s, 0, (8, 8, 8), (7, 6, 5), write)
        for ref, rows in ((f_s, (5, 6, 7)), (s1_s, (5, 6)), (s2_s, (4, 5)), (c_s, (5, 6, 7))):
            for row in rows:
                ref[row] = ref[row + 8]
        return 0

    lax.fori_loop(0, ROWS // 8, one, 0)
    for s in range(4):
        row = pl.multiple_of(lax.rem(lev_ref[0] + s, 4) * OWN + 8, 8)
        for v in range(VARS):
            part = slice(PAD * v, PAD * v + PAD)
            outs[s][:, part] = o_s[pl.ds(row + 8, 16), v]
            outs[4 + s][0:8, part] = o_s[pl.ds(row, 8), v]
            outs[4 + s][8:16, part] = o_s[pl.ds(row + 24, 8), v]


def inner(lev, fields, winds):
    arrays = (fields, *winds)
    vmem = pl.BlockSpec(memory_space=pltpu.VMEM)
    wide = pltpu.VMEM((16, VARS, PAD, NY), jnp.float32)
    return pl.pallas_call(
        inner_kernel,
        out_shape=(jax.ShapeDtypeStruct((16, 2 * PAD, NY), jnp.bfloat16),) * 8,
        in_specs=[pl.BlockSpec(memory_space=pltpu.SMEM)] + [pl.BlockSpec(memory_space=pl.ANY)] * 4,
        out_specs=(vmem,) * 8,
        scratch_shapes=[
            *[pltpu.VMEM(a.shape, jnp.float32) for a in arrays],
            wide,
            wide,
            wide,
            pltpu.VMEM((16, 5, PAD, NY), jnp.float32),
            pltpu.VMEM((ROWS + 16, VARS, PAD, NY), jnp.bfloat16),
            pltpu.SemaphoreType.DMA((4, 4)),
        ],
        compiler_params=pltpu.CompilerParams(vmem_limit_bytes=INNER_GRANT),
        name="inner",
    )(lev, *arrays)


def border_kernel(lev_ref, *refs):
    ends, halos, outs = refs[:8], refs[8:10], refs[14:18]
    f_s, s1_s, s2_s, c_s, o_s, sems = refs[18:]
    for side in range(2):
        base = 16 * side
        block = ends[4 * side : 4 * side + 4]
        own, halo_at = ((2, 0), 6) if side == 0 else ((0, 3), 0)
        for i in range(6):
            fields, winds = get_rows(block, 8, own[0] + i)
            put_fields(f_s, base + own[1] + i, fields)
            put_coefs(c_s, base + own[1] + i, winds)
        halo = halos[1 - side]
        for k in range(3):
            put_fields(f_s, base + halo_at + k, [halo[pl.ds(32 * k + PAD * v, GROUP), :] for v in range(VARS)])
        near = halo_at if side == 0 else halo_at + 1
        for k in range(2):
            put_coefs(c_s, base + near + k, [halo[pl.ds(96 + 48 * k + PAD * j, GROUP), :] for j in range(3)])
        slot = lax.rem((0 if side else 3) - lev_ref[0] + 4, 4)

        def write(i, v, value, side=side):
            o_s[side, i - 3, PAD * v : PAD * v + PAD] = masked(value)

        sweep(f_s, s1_s, s2_s, c_s, base, (7, 5, 3), (1, 2, 3), write)
        for s in range(4):

            @pl.when(slot == s)
            def _(s=s, side=side):
                rows = pl.ds(0 if side else 13, 3)
                pltpu.make_async_copy(o_s.at[side], outs[s].at[rows], sems.at[side]).start()

    for side in range(2):
        pltpu.make_async_copy(o_s.at[side], outs[0].at[pl.ds(0, 3)], sems.at[side]).wait()


def border(lev, ends, halos, sends):
    vmem = pl.BlockSpec(memory_space=pltpu.VMEM)
    wide = pltpu.VMEM((32, VARS, PAD, NY), jnp.float32)
    operands = [*ends, *halos, *sends]
    return pl.pallas_call(
        border_kernel,
        out_shape=(jax.ShapeDtypeStruct((16, 2 * PAD, NY), jnp.bfloat16),) * 4,
        in_specs=[pl.BlockSpec(memory_space=pltpu.SMEM)] + [vmem] * 10 + [pl.BlockSpec(memory_space=pl.ANY)] * 4,
        out_specs=(pl.BlockSpec(memory_space=pl.ANY),) * 4,
        input_output_aliases={11 + s: s for s in range(4)},
        scratch_shapes=[
            wide,
            wide,
            wide,
            pltpu.VMEM((32, 5, PAD, NY), jnp.float32),
            pltpu.VMEM((2, 3, 2 * PAD, NY), jnp.bfloat16),
            pltpu.SemaphoreType.DMA((2,)),
        ],
        compiler_params=pltpu.CompilerParams(vmem_limit_bytes=8 * MIB),
        name="border",
    )(lev, *operands)


def prep_kernel(lev_ref, list_ref, win_ref, wo_ref, wc_ref, winr_ref, cat_ref, wot_ref, mask_ref):
    lev = lev_ref[0]
    f32 = jnp.float32
    bf16 = jnp.bfloat16
    f_id = lax.broadcasted_iota(jnp.int32, (OUT_ROWS, 128), 1)
    o_id = lax.broadcasted_iota(jnp.int32, (OUT_ROWS, 128), 0)
    var = (f_id >= LEVELS).astype(jnp.int32) + (f_id >= 2 * LEVELS).astype(jnp.int32)
    u = (o_id == f_id + 4 * var).astype(f32).astype(bf16)
    k_id = lax.broadcasted_iota(jnp.int32, (OUT_ROWS, KEYS), 1)
    o_id = lax.broadcasted_iota(jnp.int32, (OUT_ROWS, KEYS), 0)
    source = (lev - (k_id >> 5) + 4) & 3
    level = source * GROUP + (k_id & 15)
    row = ((k_id >> 4) & 1) * 64 + level
    inner = (k_id < 128) & ((k_id & 15) < GROUP) & (o_id == row)
    edge = (k_id >= 128) & (o_id == k_id)
    r = (inner | edge).astype(f32).astype(bf16)
    nt = (((1,), (1,)), ((), ()))
    tn = (((0,), (0,)), ((), ()))
    ur = lax.dot_general(u, r, tn, preferred_element_type=f32).astype(bf16)
    winr_ref[...] = (0.5 * lax.dot_general(ur, win_ref[...], tn, preferred_element_type=f32)).astype(bf16)
    clear = lax.dot_general(wc_ref[...], ur, tn, preferred_element_type=f32).astype(bf16)
    cat_ref[0:OUT_ROWS] = jnp.dot(u, clear, preferred_element_type=f32).astype(bf16)
    cat_ref[OUT_ROWS:] = r[0:128]
    wot_ref[...] = lax.dot_general(u, wo_ref[...], nt, preferred_element_type=f32).astype(bf16)
    e = list_ref[...]
    hi = lax.broadcasted_iota(jnp.int32, (OWN, e.shape[1]), 0) == (e >> 7)
    lo = lax.broadcasted_iota(jnp.int32, (128, e.shape[1]), 0) == (e & 127)
    mask_ref[...] = lax.dot_general(
        hi.astype(f32).astype(bf16), lo.astype(f32).astype(bf16), nt, preferred_element_type=f32
    )


def prep(lev, cloud_list, input_weight, output_weight, clear_weight):
    vmem = pl.BlockSpec(memory_space=pltpu.VMEM)
    return pl.pallas_call(
        prep_kernel,
        out_shape=(
            jax.ShapeDtypeStruct((KEYS, HID), jnp.bfloat16),
            jax.ShapeDtypeStruct((OUT_ROWS + 128, KEYS), jnp.bfloat16),
            jax.ShapeDtypeStruct((OUT_ROWS, HID), jnp.bfloat16),
            jax.ShapeDtypeStruct((OWN, 128), jnp.float32),
        ),
        in_specs=[pl.BlockSpec(memory_space=pltpu.SMEM)] + [vmem] * 4,
        out_specs=(vmem,) * 4,
        compiler_params=pltpu.CompilerParams(vmem_limit_bytes=8 << 20),
        name="prep",
    )(lev, cloud_list.reshape(1, -1), input_weight, output_weight, clear_weight)


def physics_kernel(starts, g0, g1, g2, g3, surf_ref, win_ref, cat_ref, wot_ref, mask_ref, wh_hbm, *rest):
    out_hbm, surf_hbm, wh_ref, s_ref, b_ref, out_ref, surf_out_ref, wh_sem, out_sem = rest[-9:]
    f32 = jnp.float32
    bf16 = jnp.bfloat16
    layers = wh_ref.shape[0]
    fetch = [pltpu.make_async_copy(wh_hbm.at[l], wh_ref.at[l], wh_sem.at[l]) for l in range(layers)]
    for copy in fetch:
        copy.start()
    xs = []

    def act(a):
        return a + a * jnp.tanh(a)

    for h in range(2):
        pieces = [jnp.concatenate([g[8 * h + k] for k in range(8)], axis=1) for g in (g0, g1, g2, g3)]
        sf = surf_ref[:, starts[h] * NY : starts[h] * NY + HALF]
        pieces.append(jnp.concatenate([sf, jnp.zeros_like(sf)], axis=0).astype(bf16))
        x = jnp.concatenate(pieces, axis=0)
        xs.append(x)
        a = lax.dot_general(x, win_ref[...], (((0,), (0,)), ((), ())), preferred_element_type=f32)
        s = act(a)
        s_ref[h] = s
        b_ref[0, h] = s.astype(bf16) * bf16(0.5)
    for l in range(layers):
        fetch[l].wait()
        for h in range(2):
            a = jnp.dot(b_ref[l % 2, h], wh_ref[l], preferred_element_type=f32)
            s = s_ref[h] + act(a)
            if l + 1 < layers:
                s_ref[h] = s
                b_ref[(l + 1) % 2, h] = s.astype(bf16) * bf16(0.5)
            else:
                b_ref[(l + 1) % 2, h] = s.astype(bf16)
    sends = []
    for h in range(2):
        cols = slice(starts[h] * NY, starts[h] * NY + HALF)
        o = lax.dot_general(
            wot_ref[...], b_ref[layers % 2, h], (((1,), (1,)), ((), ())), preferred_element_type=f32
        )
        o = o.astype(bf16).astype(f32)
        tail = jnp.dot(cat_ref[...], xs[h], preferred_element_type=f32)
        keep = jnp.concatenate([mask_ref[starts[h] + k : starts[h] + k + 1] for k in range(8)], axis=1)
        tend = (tail[0:OUT_ROWS] + jnp.where(keep > 0.5, o, 0.0)).astype(bf16).astype(f32)
        total = tail[OUT_ROWS:] + tend[0:128]
        flat = out_ref.at[h].reshape(LEVELS * 16, NY)
        for k in range(8):
            for v in range(VARS):
                at = pl.ds(VARS * k + v, LEVELS, stride=16)
                flat[at, :] = total[64 * v : 64 * v + LEVELS, NY * k : NY * k + NY]
        surf_out_ref[h] = surf_ref[:, cols] + tend[128:]
        sends.append(pltpu.make_async_copy(out_ref.at[h], out_hbm.at[:, pl.ds(VARS * starts[h], 16)], out_sem.at[0, h]))
        sends.append(pltpu.make_async_copy(surf_out_ref.at[h], surf_hbm.at[:, cols], out_sem.at[1, h]))
        sends[-2].start()
        sends[-1].start()
    for copy in sends:
        copy.wait()


def physics(starts, got, surface, win, cat, wot, mask, wh, previous):
    vmem = pl.BlockSpec(memory_space=pltpu.VMEM)
    raw = pl.BlockSpec(memory_space=pl.ANY)
    operands = [*got, surface, win, cat, wot, mask, wh]
    in_specs = [vmem] * 9 + [raw]
    aliases = {}
    if previous is not None:
        aliases = {len(operands): 0, len(operands) + 1: 1}
        in_specs += [raw] * 2
        operands += list(previous)
    columns = surface.shape[1]
    return pl.pallas_call(
        functools.partial(physics_kernel, starts),
        out_shape=(
            jax.ShapeDtypeStruct((LEVELS, VARS * columns // NY, NY), jnp.float32),
            jax.ShapeDtypeStruct((SURF, columns), jnp.float32),
        ),
        in_specs=in_specs,
        out_specs=(raw, raw),
        scratch_shapes=[
            pltpu.VMEM(wh.shape, jnp.bfloat16),
            pltpu.VMEM((2, HALF, HID), jnp.float32),
            pltpu.VMEM((2, 2, HALF, HID), jnp.bfloat16),
            pltpu.VMEM((2, LEVELS, 16, NY), jnp.float32),
            pltpu.VMEM((2, SURF, HALF), jnp.float32),
            pltpu.SemaphoreType.DMA((wh.shape[0],)),
            pltpu.SemaphoreType.DMA((2, 2)),
        ],
        input_output_aliases=aliases,
        compiler_params=pltpu.CompilerParams(vmem_limit_bytes=30 * MIB),
        name="physics",
    )(*operands)


def step(
    fields,
    wind_x,
    wind_y,
    diffusivity,
    surface,
    cloud_list,
    input_weight,
    hidden_weight,
    output_weight,
    clear_weight,
):
    tiles = lax.axis_size("tile")
    levs = lax.axis_size("lev")
    lev = lax.axis_index("lev").astype(jnp.int32).reshape(1)

    fields = fields.reshape(-1, *fields.shape[2:])
    winds = (wind_x, wind_y, diffusivity)
    above, below, *ends = edges(fields, winds)
    lo = lax.ppermute(above, "tile", ring(tiles, 1))
    hi = lax.ppermute(below, "tile", ring(tiles, -1))
    sends = inner(lev, fields, winds)
    sends = [sends[:4], border(lev, ends, (lo, hi), sends[4:])]
    win, cat, wot, mask = prep(lev, cloud_list, input_weight, output_weight, clear_weight)
    out = None
    for starts, send in zip(CHUNKS, sends):
        got = [send[0]] + [lax.ppermute(send[s], "lev", ring(levs, s)) for s in range(1, levs)]
        out = physics(starts, got, surface, win, cat, wot, mask, hidden_weight, out)
    fields_out = out[0].reshape(LEVELS, -1, VARS, NY).transpose(2, 0, 1, 3).reshape(VARS, LEVELS, -1)
    return fields_out, out[1]


def solution(mesh):
    return jax.shard_map(
        step,
        mesh=mesh,
        in_specs=(
            P(None, "lev", "tile", None),
            P("lev", "tile", None),
            P("lev", "tile", None),
            P("lev", "tile", None),
            P(None, ("tile", "lev")),
            P(("tile", "lev")),
            P(),
            P(),
            P(),
            P(),
        ),
        out_specs=(P(None, None, ("tile", "lev")), P(None, ("tile", "lev"))),
        check_vma=False,
    )
```

```python
import functools

import jax
import jax.numpy as jnp
from jax import lax
from jax.experimental import pallas as pl
from jax.experimental.pallas import tpu as pltpu
from jax.sharding import PartitionSpec as P


VARS = 2
GROUP = 15
LEVELS = 60
SURF = 8
ROWS = 128
NY = 128
OWN = 32
PAD = 16
HID = 512
HALF = 1024
OUT_ROWS = 136
KEYS = 144
CHUNKS = ((8, 16), (0, 24))
HALO = 192
MIB = 1 << 20
EDGES_GRANT = 60 * MIB
INNER_GRANT = 52 * MIB
AHEAD = 10


def ring(count, shift):
    return [(i, (i + shift) % count) for i in range(count)]


def edges_kernel(*refs):
    arrays, halos, buffers, sems = refs[:4], refs[4:6], refs[6:14], refs[14]
    copies = []
    for side in range(2):
        for k, a in enumerate(arrays):
            rows = pl.ds(0 if side else ROWS - 8, 8)
            copies.append(pltpu.make_async_copy(a.at[:, rows], buffers[4 * side + k], sems.at[4 * side + k]))
    for copy in copies:
        copy.start()
    for copy in copies:
        copy.wait()
    for side in range(2):
        fields, winds, out = buffers[4 * side], buffers[4 * side + 1 : 4 * side + 4], halos[side]
        far, near = (5, 6) if side == 0 else (0, 0)
        flat = fields.reshape(VARS * GROUP * 8, NY)
        for k in range(3):
            for v in range(VARS):
                at = 32 * k + PAD * v
                out[at : at + GROUP] = flat[pl.ds(v * GROUP * 8 + far + k, GROUP, stride=8), :]
        for j, wind in enumerate(winds):
            flat = wind.reshape(GROUP * 8, NY)
            for k in range(2):
                at = 96 + 48 * k + PAD * j
                out[at : at + GROUP] = flat[pl.ds(near + k, GROUP, stride=8), :]


def edges(fields, winds):
    arrays = (fields, *winds)
    vmem = pl.BlockSpec(memory_space=pltpu.VMEM)
    halo = jax.ShapeDtypeStruct((HALO, NY), jnp.float32)
    ends = [jax.ShapeDtypeStruct((a.shape[0], 8, NY), jnp.float32) for a in arrays + arrays]
    return pl.pallas_call(
        edges_kernel,
        out_shape=(halo, halo, *ends),
        in_specs=[pl.BlockSpec(memory_space=pl.ANY)] * 4,
        out_specs=(vmem,) * 10,
        scratch_shapes=[pltpu.SemaphoreType.DMA((8,))],
        compiler_params=pltpu.CompilerParams(vmem_limit_bytes=EDGES_GRANT),
        name="edges",
    )(*arrays)


def coefs_of(wx, wy, d):
    lane = lax.broadcasted_iota(jnp.int32, (GROUP, NY), 1)
    hx = 0.5 * wx
    hy = 0.5 * wy
    north = jnp.where(lane == NY - 1, 0.0, d - hy)
    south = jnp.where(lane == 0, 0.0, d + hy)
    return d - hx, d + hx, north, south, 4.0 * d


def put_coefs(c_s, i, winds):
    for k, c in enumerate(coefs_of(*winds)):
        c_s[i, k, 0:GROUP] = c


def get_rows(refs, rows, x):
    flat = refs[0].reshape(VARS * GROUP * rows, NY)
    fields = [flat[pl.ds(v * GROUP * rows + x, GROUP, stride=rows), :] for v in range(VARS)]
    winds = [w.reshape(GROUP * rows, NY)[pl.ds(x, GROUP, stride=rows), :] for w in refs[1:]]
    return fields, winds


def put_fields(f_s, i, fields):
    for v in range(VARS):
        f_s[i, v, 0:GROUP] = fields[v]


def rate(cs, west, mid, east):
    total = cs[0] * east + cs[1] * west
    total = total + cs[2] * pltpu.roll(mid, NY - 1, 1) + cs[3] * pltpu.roll(mid, 1, 1)
    return total - cs[4] * mid


def sweep(f_s, s1_s, s2_s, c_s, base, count, first, write):
    levels = ((f_s, s1_s, 1.0 / 3.0), (s1_s, s2_s, 0.5), (s2_s, None, 1.0))
    for stage, (src, dst, scale) in enumerate(levels):
        low, high = first[stage], first[stage] + count[stage]
        held = {}

        def row(i, v):
            if (i, v) not in held:
                held[i, v] = src[base + i, v]
            return held[i, v]

        for i in range(low, high):
            cs = [c_s[base + i, k] for k in range(5)]
            for v in range(VARS):
                value = rate(cs, row(i - 1, v), row(i, v), row(i + 1, v))
                if scale != 1.0:
                    value = value * scale
                value = f_s[base + i, v] + value
                if dst is None:
                    write(i, v, value)
                else:
                    dst[base + i, v] = value
                held.pop((i - 1, v))


def masked(value):
    ok = lax.broadcasted_iota(jnp.int32, (PAD, NY), 0) < GROUP
    return jnp.where(ok, value, 0.0).astype(jnp.bfloat16)


def inner_kernel(lev_ref, *refs):
    arrays, outs, buffers = refs[:4], refs[4:12], refs[12:16]
    f_s, s1_s, s2_s, c_s, o_s, sems = refs[16:]
    blocks = ROWS // 8

    def copies(block):
        rows = pl.ds(pl.multiple_of(block * 8, 8), 8)
        return [
            pltpu.make_async_copy(a.at[:, rows], b.at[block], sems.at[block, k])
            for k, (a, b) in enumerate(zip(arrays, buffers))
        ]

    for block in range(AHEAD):
        for copy in copies(block):
            copy.start()

    def one(block, _):
        for copy in copies(block):
            copy.wait()

        @pl.when(block + AHEAD < blocks)
        def _():
            for copy in copies(block + AHEAD):
                copy.start()

        base = 8 * block
        for i in range(8):
            fields, winds = get_rows([b.at[block] for b in buffers], 8, i)
            put_fields(f_s, 8 + i, fields)
            put_coefs(c_s, 8 + i, winds)

        def write(i, v, value):
            o_s[base + i, v] = masked(value)

        sweep(f_s, s1_s, s2_s, c_s, 0, (8, 8, 8), (7, 6, 5), write)
        for ref, rows in ((f_s, (5, 6, 7)), (s1_s, (5, 6)), (s2_s, (4, 5)), (c_s, (5, 6, 7))):
            for row in rows:
                ref[row] = ref[row + 8]
        return 0

    lax.fori_loop(0, blocks, one, 0)
    for s in range(4):
        row = pl.multiple_of(lax.rem(lev_ref[0] + s, 4) * OWN + 8, 8)
        for v in range(VARS):
            part = slice(PAD * v, PAD * v + PAD)
            outs[s][:, part] = o_s[pl.ds(row + 8, 16), v]
            outs[4 + s][0:8, part] = o_s[pl.ds(row, 8), v]
            outs[4 + s][8:16, part] = o_s[pl.ds(row + 24, 8), v]


def inner(lev, fields, winds):
    arrays = (fields, *winds)
    vmem = pl.BlockSpec(memory_space=pltpu.VMEM)
    wide = pltpu.VMEM((16, VARS, PAD, NY), jnp.float32)
    return pl.pallas_call(
        inner_kernel,
        out_shape=(jax.ShapeDtypeStruct((16, 2 * PAD, NY), jnp.bfloat16),) * 8,
        in_specs=[pl.BlockSpec(memory_space=pltpu.SMEM)] + [pl.BlockSpec(memory_space=pl.ANY)] * 4,
        out_specs=(vmem,) * 8,
        scratch_shapes=[
            *[pltpu.VMEM((ROWS // 8, a.shape[0], 8, NY), jnp.float32) for a in arrays],
            wide,
            wide,
            wide,
            pltpu.VMEM((16, 5, PAD, NY), jnp.float32),
            pltpu.VMEM((ROWS + 16, VARS, PAD, NY), jnp.bfloat16),
            pltpu.SemaphoreType.DMA((ROWS // 8, 4)),
        ],
        compiler_params=pltpu.CompilerParams(vmem_limit_bytes=INNER_GRANT),
        name="inner",
    )(lev, *arrays)


def border_kernel(lev_ref, *refs):
    ends, halos, outs = refs[:8], refs[8:10], refs[14:18]
    f_s, s1_s, s2_s, c_s, o_s, sems = refs[18:]
    for side in range(2):
        base = 16 * side
        block = ends[4 * side : 4 * side + 4]
        own, halo_at = ((2, 0), 6) if side == 0 else ((0, 3), 0)
        for i in range(6):
            fields, winds = get_rows(block, 8, own[0] + i)
            put_fields(f_s, base + own[1] + i, fields)
            put_coefs(c_s, base + own[1] + i, winds)
        halo = halos[1 - side]
        for k in range(3):
            put_fields(f_s, base + halo_at + k, [halo[pl.ds(32 * k + PAD * v, GROUP), :] for v in range(VARS)])
        near = halo_at if side == 0 else halo_at + 1
        for k in range(2):
            put_coefs(c_s, base + near + k, [halo[pl.ds(96 + 48 * k + PAD * j, GROUP), :] for j in range(3)])
        slot = lax.rem((0 if side else 3) - lev_ref[0] + 4, 4)

        def write(i, v, value, side=side):
            o_s[side, i - 3, PAD * v : PAD * v + PAD] = masked(value)

        sweep(f_s, s1_s, s2_s, c_s, base, (7, 5, 3), (1, 2, 3), write)
        for s in range(4):

            @pl.when(slot == s)
            def _(s=s, side=side):
                rows = pl.ds(0 if side else 13, 3)
                pltpu.make_async_copy(o_s.at[side], outs[s].at[rows], sems.at[side]).start()

    for side in range(2):
        pltpu.make_async_copy(o_s.at[side], outs[0].at[pl.ds(0, 3)], sems.at[side]).wait()


def border(lev, ends, halos, sends):
    vmem = pl.BlockSpec(memory_space=pltpu.VMEM)
    wide = pltpu.VMEM((32, VARS, PAD, NY), jnp.float32)
    operands = [*ends, *halos, *sends]
    return pl.pallas_call(
        border_kernel,
        out_shape=(jax.ShapeDtypeStruct((16, 2 * PAD, NY), jnp.bfloat16),) * 4,
        in_specs=[pl.BlockSpec(memory_space=pltpu.SMEM)] + [vmem] * 10 + [pl.BlockSpec(memory_space=pl.ANY)] * 4,
        out_specs=(pl.BlockSpec(memory_space=pl.ANY),) * 4,
        input_output_aliases={11 + s: s for s in range(4)},
        scratch_shapes=[
            wide,
            wide,
            wide,
            pltpu.VMEM((32, 5, PAD, NY), jnp.float32),
            pltpu.VMEM((2, 3, 2 * PAD, NY), jnp.bfloat16),
            pltpu.SemaphoreType.DMA((2,)),
        ],
        compiler_params=pltpu.CompilerParams(vmem_limit_bytes=8 * MIB),
        name="border",
    )(lev, *operands)


def prep_kernel(lev_ref, list_ref, win_ref, wo_ref, wc_ref, winr_ref, cat_ref, wot_ref, mask_ref):
    lev = lev_ref[0]
    f32 = jnp.float32
    bf16 = jnp.bfloat16
    f_id = lax.broadcasted_iota(jnp.int32, (OUT_ROWS, 128), 1)
    o_id = lax.broadcasted_iota(jnp.int32, (OUT_ROWS, 128), 0)
    var = (f_id >= LEVELS).astype(jnp.int32) + (f_id >= 2 * LEVELS).astype(jnp.int32)
    u = (o_id == f_id + 4 * var).astype(f32).astype(bf16)
    k_id = lax.broadcasted_iota(jnp.int32, (OUT_ROWS, KEYS), 1)
    o_id = lax.broadcasted_iota(jnp.int32, (OUT_ROWS, KEYS), 0)
    source = (lev - (k_id >> 5) + 4) & 3
    level = source * GROUP + (k_id & 15)
    row = ((k_id >> 4) & 1) * 64 + level
    inner = (k_id < 128) & ((k_id & 15) < GROUP) & (o_id == row)
    edge = (k_id >= 128) & (o_id == k_id)
    r = (inner | edge).astype(f32).astype(bf16)
    nt = (((1,), (1,)), ((), ()))
    tn = (((0,), (0,)), ((), ()))
    ur = lax.dot_general(u, r, tn, preferred_element_type=f32).astype(bf16)
    winr_ref[...] = (0.5 * lax.dot_general(ur, win_ref[...], tn, preferred_element_type=f32)).astype(bf16)
    clear = lax.dot_general(wc_ref[...], ur, tn, preferred_element_type=f32).astype(bf16)
    cat_ref[0:OUT_ROWS] = jnp.dot(u, clear, preferred_element_type=f32).astype(bf16)
    cat_ref[OUT_ROWS:] = r[0:128]
    wot_ref[...] = lax.dot_general(u, wo_ref[...], nt, preferred_element_type=f32).astype(bf16)
    e = list_ref[...]
    hi = lax.broadcasted_iota(jnp.int32, (OWN, e.shape[1]), 0) == (e >> 7)
    lo = lax.broadcasted_iota(jnp.int32, (128, e.shape[1]), 0) == (e & 127)
    mask_ref[...] = lax.dot_general(
        hi.astype(f32).astype(bf16), lo.astype(f32).astype(bf16), nt, preferred_element_type=f32
    )


def prep(lev, cloud_list, input_weight, output_weight, clear_weight):
    vmem = pl.BlockSpec(memory_space=pltpu.VMEM)
    return pl.pallas_call(
        prep_kernel,
        out_shape=(
            jax.ShapeDtypeStruct((KEYS, HID), jnp.bfloat16),
            jax.ShapeDtypeStruct((OUT_ROWS + 128, KEYS), jnp.bfloat16),
            jax.ShapeDtypeStruct((OUT_ROWS, HID), jnp.bfloat16),
            jax.ShapeDtypeStruct((OWN, 128), jnp.float32),
        ),
        in_specs=[pl.BlockSpec(memory_space=pltpu.SMEM)] + [vmem] * 4,
        out_specs=(vmem,) * 4,
        compiler_params=pltpu.CompilerParams(vmem_limit_bytes=8 << 20),
        name="prep",
    )(lev, cloud_list.reshape(1, -1), input_weight, output_weight, clear_weight)


def physics_kernel(starts, g0, g1, g2, g3, surf_ref, win_ref, cat_ref, wot_ref, mask_ref, wh_hbm, *rest):
    out_hbm, surf_hbm, wh_ref, s_ref, b_ref, out_ref, surf_out_ref, wh_sem, out_sem = rest[-9:]
    f32 = jnp.float32
    bf16 = jnp.bfloat16
    layers = wh_ref.shape[0]
    fetch = [pltpu.make_async_copy(wh_hbm.at[l], wh_ref.at[l], wh_sem.at[l]) for l in range(layers)]
    for copy in fetch:
        copy.start()
    xs = []

    def act(a):
        return a + a * jnp.tanh(a)

    for h in range(2):
        pieces = [jnp.concatenate([g[8 * h + k] for k in range(8)], axis=1) for g in (g0, g1, g2, g3)]
        sf = surf_ref[:, starts[h] * NY : starts[h] * NY + HALF]
        pieces.append(jnp.concatenate([sf, jnp.zeros_like(sf)], axis=0).astype(bf16))
        x = jnp.concatenate(pieces, axis=0)
        xs.append(x)
        a = lax.dot_general(x, win_ref[...], (((0,), (0,)), ((), ())), preferred_element_type=f32)
        s = act(a)
        s_ref[h] = s
        b_ref[0, h] = s.astype(bf16) * bf16(0.5)
    for l in range(layers):
        fetch[l].wait()
        for h in range(2):
            a = jnp.dot(b_ref[l % 2, h], wh_ref[l], preferred_element_type=f32)
            s = s_ref[h] + act(a)
            if l + 1 < layers:
                s_ref[h] = s
                b_ref[(l + 1) % 2, h] = s.astype(bf16) * bf16(0.5)
            else:
                b_ref[(l + 1) % 2, h] = s.astype(bf16)
    sends = []
    for h in range(2):
        cols = slice(starts[h] * NY, starts[h] * NY + HALF)
        o = lax.dot_general(
            wot_ref[...], b_ref[layers % 2, h], (((1,), (1,)), ((), ())), preferred_element_type=f32
        )
        o = o.astype(bf16).astype(f32)
        tail = jnp.dot(cat_ref[...], xs[h], preferred_element_type=f32)
        keep = jnp.concatenate([mask_ref[starts[h] + k : starts[h] + k + 1] for k in range(8)], axis=1)
        tend = (tail[0:OUT_ROWS] + jnp.where(keep > 0.5, o, 0.0)).astype(bf16).astype(f32)
        total = tail[OUT_ROWS:] + tend[0:128]
        flat = out_ref.at[h].reshape(LEVELS * 16, NY)
        for k in range(8):
            for v in range(VARS):
                at = pl.ds(VARS * k + v, LEVELS, stride=16)
                flat[at, :] = total[64 * v : 64 * v + LEVELS, NY * k : NY * k + NY]
        surf_out_ref[h] = surf_ref[:, cols] + tend[128:]
        sends.append(pltpu.make_async_copy(out_ref.at[h], out_hbm.at[:, pl.ds(VARS * starts[h], 16)], out_sem.at[0, h]))
        sends.append(pltpu.make_async_copy(surf_out_ref.at[h], surf_hbm.at[:, cols], out_sem.at[1, h]))
        sends[-2].start()
        sends[-1].start()
    for copy in sends:
        copy.wait()


def physics(starts, got, surface, win, cat, wot, mask, wh, previous):
    vmem = pl.BlockSpec(memory_space=pltpu.VMEM)
    raw = pl.BlockSpec(memory_space=pl.ANY)
    operands = [*got, surface, win, cat, wot, mask, wh]
    in_specs = [vmem] * 9 + [raw]
    aliases = {}
    if previous is not None:
        aliases = {len(operands): 0, len(operands) + 1: 1}
        in_specs += [raw] * 2
        operands += list(previous)
    columns = surface.shape[1]
    return pl.pallas_call(
        functools.partial(physics_kernel, starts),
        out_shape=(
            jax.ShapeDtypeStruct((LEVELS, VARS * columns // NY, NY), jnp.float32),
            jax.ShapeDtypeStruct((SURF, columns), jnp.float32),
        ),
        in_specs=in_specs,
        out_specs=(raw, raw),
        scratch_shapes=[
            pltpu.VMEM(wh.shape, jnp.bfloat16),
            pltpu.VMEM((2, HALF, HID), jnp.float32),
            pltpu.VMEM((2, 2, HALF, HID), jnp.bfloat16),
            pltpu.VMEM((2, LEVELS, 16, NY), jnp.float32),
            pltpu.VMEM((2, SURF, HALF), jnp.float32),
            pltpu.SemaphoreType.DMA((wh.shape[0],)),
            pltpu.SemaphoreType.DMA((2, 2)),
        ],
        input_output_aliases=aliases,
        compiler_params=pltpu.CompilerParams(vmem_limit_bytes=30 * MIB),
        name="physics",
    )(*operands)


def step(
    fields,
    wind_x,
    wind_y,
    diffusivity,
    surface,
    cloud_list,
    input_weight,
    hidden_weight,
    output_weight,
    clear_weight,
):
    tiles = lax.axis_size("tile")
    levs = lax.axis_size("lev")
    lev = lax.axis_index("lev").astype(jnp.int32).reshape(1)

    fields = fields.reshape(-1, *fields.shape[2:])
    winds = (wind_x, wind_y, diffusivity)
    above, below, *ends = edges(fields, winds)
    lo = lax.ppermute(above, "tile", ring(tiles, 1))
    hi = lax.ppermute(below, "tile", ring(tiles, -1))
    sends = inner(lev, fields, winds)
    sends = [sends[:4], border(lev, ends, (lo, hi), sends[4:])]
    win, cat, wot, mask = prep(lev, cloud_list, input_weight, output_weight, clear_weight)
    out = None
    for starts, send in zip(CHUNKS, sends):
        got = [send[0]] + [lax.ppermute(send[s], "lev", ring(levs, s)) for s in range(1, levs)]
        out = physics(starts, got, surface, win, cat, wot, mask, hidden_weight, out)
    fields_out = out[0].reshape(LEVELS, -1, VARS, NY).transpose(2, 0, 1, 3).reshape(VARS, LEVELS, -1)
    return fields_out, out[1]


def solution(mesh):
    return jax.shard_map(
        step,
        mesh=mesh,
        in_specs=(
            P(None, "lev", "tile", None),
            P("lev", "tile", None),
            P("lev", "tile", None),
            P("lev", "tile", None),
            P(None, ("tile", "lev")),
            P(("tile", "lev")),
            P(),
            P(),
            P(),
            P(),
        ),
        out_specs=(P(None, None, ("tile", "lev")), P(None, ("tile", "lev"))),
        check_vma=False,
    )
```
